32 devices in a mesh: facet: 8 (over y, x, core), chan: 4 (over z).
Axes of the slice: x: 2, y: 2, z: 4, core: 2. Of those that a mesh axis runs over, the one named last changes fastest.
Arguments:
- model_taylor: float32 [2, 8, 2, 512, 512], P(None, 'facet'), may hold values from -6 to 6
- channel_offset: float32 [4], P('chan'), may hold values from -0.5 to 0.5
- assignment: int32 [8], replicated, may hold values from 0 to 7, each once
- observed: float32 [4, 8, 2, 4096], P('chan', 'facet'), may hold values from -12 to 12
- uv_bins: int32 [4, 8, 4096], P('chan', 'facet'), may hold values from 0 to 16383
- vis_counts: int32 [4, 8], P('chan', 'facet'), may hold values from 1 to 4096, 16384 in all within a row
Outputs:
- taylor_residual: float32 [2, 8, 2, 512, 512], P(None, 'facet', None, 'chan')
The draws below stay inside these ranges and needn't reach their ends.
Inputs may be any that keep to these rules, and one draw needn't show every extreme that they name: A permutation: task t, held by helper t, works on subgrid assignment[t]. Slots 0 .. vis_counts - 1 of a task are live; the others are ignored.
All inputs are finite; a program needn't handle non-finite values. No bound on the sum of `vis_counts` on one device may be relied on, other than what follows from the above.
Results may differ from the reference program's by a relative error of at most 0.0003.
Values sent between devices are 32-bit elements; how exact they have to be, the bound alone decides.
A program may use at most 128 MiB of HBM per device.

```python
import math
import jax
import jax.numpy as jnp
import numpy as np
from jax import lax

FS = 512
XM = 128
FACET_COLS = 4
SUB_COLS = 4
VIS = 4096
NF = 8
NSUB = 8
CHANS = 4
IMAGE = 2048


def set_ends(entries, rng, smallest, top_value):
    longest = entries.shape.index(max(entries.shape))
    spots = []
    for shift in (0, 1):
        where = [jax.random.randint(jax.random.fold_in(rng, axis), (), 0, length) for axis, length in enumerate(entries.shape)]
        where[longest] = (where[longest] + shift) % entries.shape[longest]
        spots.append(tuple(where))
    return entries.at[spots[0]].set(smallest).at[spots[1]].set(top_value)


def block_scale(key, dims, shards, smallest, largest):
    gain = 1.0
    for position, blocks in shards:
        heights = jax.random.uniform(jax.random.fold_in(jax.random.fold_in(key, 6), position), (blocks,), jnp.float32, smallest / len(shards), largest / len(shards))
        gain = gain * jnp.repeat(jnp.exp(heights), dims[position] // blocks).reshape((-1,) + (1,) * (len(dims) - 1 - position))
    return gain


def length_profile(number_of, total, limit, lean):
    weights = [(1 << 20) // math.isqrt(rank ** lean) + 1 for rank in range(2, number_of + 1)]
    surplus, given = total - limit - (number_of - 1), [1] * (number_of - 1)
    while surplus > 0:
        candidates = [i for i in range(number_of - 1) if given[i] < limit]
        mass, budget = sum([weights[i] for i in candidates]), surplus
        for i in candidates:
            more = min(limit - given[i], max(1, budget * weights[i] // mass), surplus)
            given[i] = given[i] + more
            surplus = surplus - more
    return np.array([limit] + given)


def uneven_parts(stream_key, count, total, reach, lean):
    if count == 2:
        one = jax.random.randint(stream_key, (), max(1, total - reach), min(reach, total - 1) + 1)
        return jnp.stack([one, total - one])
    sizes = jnp.asarray(length_profile(count, total, reach, lean), jnp.int32)
    pairs = (count - 1) // 2
    donor, receiver = sizes[1:1 + 2 * pairs:2], sizes[2:2 + 2 * pairs:2]
    room = jnp.minimum(donor - 1, reach - receiver)
    shifted = jax.random.randint(jax.random.fold_in(stream_key, 1), (pairs,), 0, 1 << 20) % (room + 1)
    sizes = sizes.at[1:1 + 2 * pairs:2].set(donor - shifted).at[2:2 + 2 * pairs:2].set(receiver + shifted)
    return sizes[jax.random.permutation(jax.random.fold_in(stream_key, 2), count)]


def gaussian(rng, shape, scale, limit, pieces=(), kind=jnp.bfloat16):
    entries = scale * jax.random.normal(rng, shape, jnp.float32)
    if pieces:
        entries = entries * block_scale(rng, shape, pieces, -0.22, 0.18)
    return jnp.clip(entries, -limit, limit).astype(kind)


def setup_inputs(seed: int = 0) -> dict:
    seeds = jax.random.split(jax.random.key(seed), 7)
    model_taylor = gaussian(seeds[0], (2, NF, 2, FS, FS), 1.0, 6.0, ((1, 8),), jnp.float32)
    channel_offset = jnp.clip(jax.random.uniform(seeds[1], (CHANS,), jnp.float32, -0.5, 0.5) * block_scale(seeds[1], (CHANS,), ((0, 4),), -0.4, 0.0), -0.5, 0.5)
    assignment = jax.random.permutation(seeds[2], NSUB).astype(jnp.int32)
    observed = gaussian(seeds[3], (CHANS, NSUB, 2, VIS), 2.0, 12.0, ((0, 4), (1, 8)), jnp.float32)
    uv_bins = set_ends(jax.random.randint(seeds[4], (CHANS, NSUB, VIS), 0, XM * XM), jax.random.fold_in(seeds[4], 1), 0, (XM * XM) - 1).astype(jnp.int32)
    vis_counts = jax.vmap(lambda own: uneven_parts(own, NSUB, NSUB * VIS // 2, VIS, 2))(jax.random.split(seeds[5], CHANS)).reshape((CHANS, NSUB)).astype(jnp.int32)
    return {"model_taylor": model_taylor, "channel_offset": channel_offset, "assignment": assignment, "observed": observed, "uv_bins": uv_bins, "vis_counts": vis_counts}


TWO_PI = 6.283185307179586
HIGHEST = lax.Precision.HIGHEST

def taper_values(length):
    positions = jnp.arange(length, dtype=jnp.float32)
    shaped = 0.55 + 0.45 * jnp.cos(jnp.pi * (2.0 * positions + 1.0 - length) / length)
    return shaped / jnp.sqrt(jnp.float32(length))

def phase_pair(frequency, pixels):
    product = frequency[:, None] * pixels[None, :] % IMAGE
    angle = product.astype(jnp.float32) * (TWO_PI / IMAGE)
    return (jnp.cos(angle), -jnp.sin(angle))

def row_table(facet_row, row_total):
    frequency = jnp.arange(row_total * XM, dtype=jnp.int32)
    pixels = facet_row * FS + jnp.arange(FS, dtype=jnp.int32)
    real_part, imag_part = phase_pair(frequency, pixels)
    window = taper_values(FS)[None, :]
    return jnp.concatenate([real_part * window, imag_part * window], axis=1)

def column_table(facet_col):
    frequency = jnp.arange(SUB_COLS * XM, dtype=jnp.int32)
    pixels = facet_col * FS + jnp.arange(FS, dtype=jnp.int32)
    real_part, imag_part = phase_pair(frequency, pixels)
    window = taper_values(FS)[None, :]
    real_part = (real_part * window).reshape(SUB_COLS, XM, FS).transpose(2, 0, 1)
    imag_part = (imag_part * window).reshape(SUB_COLS, XM, FS).transpose(2, 0, 1)
    upper_rows = jnp.stack([real_part, imag_part], axis=2).reshape(FS, SUB_COLS * 2 * XM)
    lower_rows = jnp.stack([-imag_part, real_part], axis=2).reshape(FS, SUB_COLS * 2 * XM)
    return jnp.concatenate([upper_rows, lower_rows], axis=0)

def predict(sky_image, rows_tab, cols_fwd, row_total):
    joined = jnp.concatenate([sky_image[0], sky_image[1]], axis=1)
    prepared = jnp.dot(joined, cols_fwd, precision=HIGHEST, preferred_element_type=jnp.float32)
    prepared = prepared.reshape(FS, SUB_COLS, 2, XM)
    real_part = prepared[:, :, 0]
    imag_part = prepared[:, :, 1]
    upper_rows = jnp.stack([real_part, imag_part], axis=2).reshape(FS, SUB_COLS * 2 * XM)
    lower_rows = jnp.stack([-imag_part, real_part], axis=2).reshape(FS, SUB_COLS * 2 * XM)
    mixer = jnp.concatenate([upper_rows, lower_rows], axis=0)
    result = jnp.dot(rows_tab, mixer, precision=HIGHEST, preferred_element_type=jnp.float32)
    result = result.reshape(row_total, XM, SUB_COLS, 2, XM).transpose(0, 2, 3, 1, 4)
    return result.reshape(row_total * SUB_COLS, 2, XM, XM)

def adjoint_rows(rows_tab, row_total):
    return rows_tab.reshape(row_total * XM, 2, FS).transpose(1, 0, 2).reshape(2 * row_total * XM, FS)

def adjoint(uv_grids, rows_adj, cols_adj, row_total):
    arranged = uv_grids.reshape(row_total, SUB_COLS, 2, XM, XM).transpose(0, 3, 1, 2, 4)
    upper_rows = arranged.reshape(row_total * XM, SUB_COLS * 2 * XM)
    lower_rows = jnp.stack([arranged[:, :, :, 1], -arranged[:, :, :, 0]], axis=3)
    lower_rows = lower_rows.reshape(row_total * XM, SUB_COLS * 2 * XM)
    mixer = jnp.concatenate([upper_rows, lower_rows], axis=0)
    weighted = lax.dot_general(rows_adj, mixer, (((0,), (0,)), ((), ())), precision=HIGHEST, preferred_element_type=jnp.float32)
    joined = jnp.dot(weighted, cols_adj, precision=HIGHEST, preferred_element_type=jnp.float32)
    return joined.reshape(joined.shape[0], 2, FS).transpose(1, 0, 2)

def residual_grid(uv_grid, observed_one, cell_index, live_total):
    flat_grid = uv_grid.reshape(2, XM * XM)
    predicted = jnp.take(flat_grid, cell_index, axis=1)
    is_live = jnp.arange(cell_index.shape[0], dtype=jnp.int32) < live_total
    misfit = jnp.where(is_live[None, :], observed_one - predicted, 0.0)
    return jnp.zeros_like(flat_grid).at[:, cell_index].add(misfit).reshape(2, XM, XM)

def reference(model_taylor, channel_offset, assignment, observed, uv_bins, vis_counts):
    row_total = NSUB // SUB_COLS
    facet_ids = jnp.arange(NF, dtype=jnp.int32)

    def forward(running, facet_index):
        rows_tab = row_table(facet_index // FACET_COLS, row_total)
        cols_fwd = column_table(facet_index % FACET_COLS)
        terms = lax.dynamic_index_in_dim(model_taylor, facet_index, 1, keepdims=False)
        parts = jnp.stack([predict(terms[0], rows_tab, cols_fwd, row_total), predict(terms[1], rows_tab, cols_fwd, row_total)])
        return (running + parts, None)
    summed, _ = lax.scan(forward, jnp.zeros((2, NSUB, 2, XM, XM), jnp.float32), facet_ids)
    uv_grids = summed[0][None] + channel_offset[:, None, None, None, None] * summed[1][None]
    by_task = jnp.take(uv_grids, assignment, axis=1)
    misfits = jax.vmap(jax.vmap(residual_grid))(by_task, observed, uv_bins, vis_counts)
    ordered = jnp.zeros_like(misfits).at[:, assignment].set(misfits)
    weights = jnp.stack([jnp.ones_like(channel_offset), channel_offset])
    taylor = jnp.einsum('tc,csabk->tsabk', weights, ordered, precision=HIGHEST)

    def backward(facet_index):
        rows_adj = adjoint_rows(row_table(facet_index // FACET_COLS, row_total), row_total)
        cols_adj = column_table(facet_index % FACET_COLS).T
        return jnp.stack([adjoint(taylor[0], rows_adj, cols_adj, row_total), adjoint(taylor[1], rows_adj, cols_adj, row_total)])
    result = lax.map(backward, facet_ids)
    return jnp.transpose(result, (1, 0, 2, 3, 4))
```

```python
import functools

import jax
import jax.numpy as jnp
from jax import lax
from jax.experimental import pallas as pl
from jax.experimental.pallas import tpu as pltpu
from jax.sharding import PartitionSpec as P

XM = 128
FACET_COLS = 4
SUB_COLS = 4
IMAGE = 2048
TWO_PI = 6.283185307179586
F32 = jnp.float32
BF16 = jnp.bfloat16
MESH = pl.DeviceIdType.MESH
VMEM_SPEC = pl.BlockSpec(memory_space=pltpu.VMEM)
SMEM_SPEC = pl.BlockSpec(memory_space=pltpu.SMEM)
VMEM_LIMIT = 56 * 1024 * 1024


def cos_sin(turns):
    quarter = IMAGE // 4
    shift = quarter.bit_length() - 1
    step = (turns + quarter // 2) >> shift
    rest = turns - (step << shift)
    t = rest.astype(F32) * (TWO_PI / IMAGE)
    t2 = t * t
    s = t * (1.0 + t2 * (-1.0 / 6 + t2 * (1.0 / 120 + t2 * (-1.0 / 5040 + t2 * (1.0 / 362880)))))
    c = 1.0 + t2 * (-0.5 + t2 * (1.0 / 24 + t2 * (-1.0 / 720 + t2 * (1.0 / 40320))))
    odd = (step & 1) == 1
    cos = jnp.where(odd, s, c)
    sin = jnp.where(odd, c, s)
    cos = jnp.where(((step + 1) & 2) == 2, -cos, cos)
    sin = jnp.where((step & 2) == 2, -sin, sin)
    return cos, sin


def window(positions, length):
    cos, _ = cos_sin(((2 * positions + 1 - length) * (IMAGE // (2 * length))) & (IMAGE - 1))
    return (0.55 + 0.45 * cos) * (float(length) ** -0.5)


def phases(frequency, pixel):
    cos, sin = cos_sin((frequency * pixel) & (IMAGE - 1))
    return cos, -sin


def split(value):
    high = value.astype(BF16)
    return high, (value - high.astype(F32)).astype(BF16)


def put(high_ref, low_ref, where, value):
    high, low = split(value)
    high_ref[where] = high
    low_ref[where] = low


def dot3(a_high, a_low, b_high, b_low):
    dot = functools.partial(jnp.dot, preferred_element_type=F32)
    return dot(a_high, b_high) + (dot(a_low, b_high) + dot(a_high, b_low))


def iota(shape, dim):
    return lax.broadcasted_iota(jnp.int32, shape, dim)


def predict_kernel(subs, rel_ref, pos_ref, off_ref, model_ref, out_ref, bh, bl, ah, al, mh, ml, ph, plo, grid):
    xb, fs = model_ref.shape[3:]
    cells = SUB_COLS * XM
    total = subs // SUB_COLS * XM
    i = pl.program_id(0)
    row_pix, col_pix = pos_ref[0] * fs, pos_ref[1] * fs

    @pl.when(i == 0)
    def _():
        grid[...] = jnp.zeros_like(grid)
        chunk = 64

        @pl.loop(0, fs // chunk)
        def _(k):
            base = pl.multiple_of(k * chunk, chunk)
            y = base + iota((chunk, cells), 0)
            re, im = phases(iota((chunk, cells), 1), col_pix + y)
            w = window(base + iota((chunk, XM), 0), fs)[:, :1]
            re, im = re * w, im * w
            top, low = pl.ds(base, chunk), pl.ds(pl.multiple_of(fs + base, chunk), chunk)
            put(bh, bl, (top, slice(0, cells)), re)
            put(bh, bl, (top, slice(cells, 2 * cells)), im)
            put(bh, bl, (low, slice(0, cells)), -im)
            put(bh, bl, (low, slice(cells, 2 * cells)), re)

    chunk = 64

    @pl.loop(0, total // chunk)
    def _(k):
        base = pl.multiple_of(k * chunk, chunk)
        x = i * xb + iota((chunk, xb), 1)
        re, im = phases(base + iota((chunk, xb), 0), row_pix + x)
        w = window(i * xb + iota((8, xb), 1), fs)[:1]
        rows = pl.ds(base, chunk)
        put(ah, al, (rows, slice(0, xb)), re * w)
        put(ah, al, (rows, slice(xb, 2 * xb)), im * w)

    offset = off_ref[0]
    for p in range(2):
        value = model_ref[0, 0, p] + offset * model_ref[1, 0, p]
        put(mh, ml, (slice(None), slice(p * fs, (p + 1) * fs)), value)

    tile = 256
    for k in range(2 * cells // tile):
        cols = slice(k * tile, (k + 1) * tile)
        part = dot3(mh[...], ml[...], bh[:, cols], bl[:, cols])
        high, low = split(part)
        ph[:xb, cols] = high
        plo[:xb, cols] = low
        if k * tile < cells:
            other = slice(k * tile + cells, (k + 1) * tile + cells)
        else:
            other = slice(k * tile - cells, (k + 1) * tile - cells)
            high, low = -high, -low
        ph[xb:, other] = high
        plo[xb:, other] = low
    for k in range(2 * cells // tile):
        cols = slice(k * tile, (k + 1) * tile)
        grid[:, cols] += dot3(ah[...], al[...], ph[:, cols], plo[:, cols])

    @pl.when(i == pl.num_programs(0) - 1)
    def _():
        for s in range(subs):
            a, b = s // SUB_COLS, s % SUB_COLS
            for p in range(2):
                out_ref[rel_ref[s], p] = grid[a * XM:(a + 1) * XM, p * cells + b * XM:p * cells + (b + 1) * XM]


def predict(subs, rel, pos, offset, model):
    fs = model.shape[-1]
    xb = fs // 2
    cells = SUB_COLS * XM
    total = subs // SUB_COLS * XM
    return pl.pallas_call(
        functools.partial(predict_kernel, subs),
        out_shape=jax.ShapeDtypeStruct((subs, 2, XM, XM), F32),
        grid=(fs // xb,),
        in_specs=[SMEM_SPEC] * 3 + [pl.BlockSpec((2, 1, 2, xb, fs), lambda i: (0, 0, 0, i, 0))],
        out_specs=pl.BlockSpec((subs, 2, XM, XM), lambda i: (0, 0, 0, 0)),
        scratch_shapes=[
            pltpu.VMEM((2 * fs, 2 * cells), BF16),
            pltpu.VMEM((2 * fs, 2 * cells), BF16),
            pltpu.VMEM((total, 2 * xb), BF16),
            pltpu.VMEM((total, 2 * xb), BF16),
            pltpu.VMEM((xb, 2 * fs), BF16),
            pltpu.VMEM((xb, 2 * fs), BF16),
            pltpu.VMEM((2 * xb, 2 * cells), BF16),
            pltpu.VMEM((2 * xb, 2 * cells), BF16),
            pltpu.VMEM((total, 2 * cells), F32),
        ],
        compiler_params=pltpu.CompilerParams(vmem_limit_bytes=VMEM_LIMIT),
    )(rel, pos, offset, model)


def flipped(me, bit):
    size = 1 << bit
    return me + (1 - 2 * ((me // size) % 2)) * size


def reduce_kernel(bits, in_ref, out_ref, acc, recv, send_sem, recv_sem):
    me = lax.axis_index("facet")
    barrier = pltpu.get_barrier_semaphore()
    for b in range(bits):
        pl.semaphore_signal(barrier, inc=1, device_id={"facet": flipped(me, b)}, device_id_type=MESH)
    pl.semaphore_wait(barrier, bits)

    orders = [[0] + list(range(1, bits)), [0] + list(range(bits - 1, 0, -1))]
    source = {(r, p): in_ref for r in range(1 << bits) for p in range(2)}
    copies = {}

    def send(r, p, bit):
        copy = pltpu.make_async_remote_copy(
            src_ref=source[r, p].at[r, p],
            dst_ref=recv.at[r, p],
            send_sem=send_sem.at[r, p],
            recv_sem=recv_sem.at[r, p],
            device_id={"facet": flipped(me, bit)},
            device_id_type=MESH,
        )
        copy.start()
        copies[r, p] = copy

    def ranked(members, later):
        return sorted(members, key=lambda r: [-((r >> b) & 1) for b in later])

    members = [list(range(1 << bits)) for _ in range(2)]
    firsts = [ranked([r for r in members[p] if (r >> orders[p][0]) & 1], orders[p][1:]) for p in range(2)]
    for pair in zip(*firsts):
        for p in range(2):
            send(pair[p], p, orders[p][0])
    for i in range(bits):
        kept = []
        for p in range(2):
            bit = orders[p][i]
            members[p] = ranked([r for r in members[p] if not (r >> bit) & 1], orders[p][i + 1:])
            kept.append(members[p])
        for pair in zip(*kept):
            for p in range(2):
                r, bit = pair[p], orders[p][i]
                copies[r | (1 << bit), p].wait_recv()
                value = source[r, p][r, p] + recv[r | (1 << bit), p]
                if i == bits - 1:
                    out_ref[p] = value
                else:
                    acc[r, p] = value
                    source[r, p] = acc
                    if (r >> orders[p][i + 1]) & 1:
                        send(r, p, orders[p][i + 1])
    for copy in copies.values():
        copy.wait_send()


def reduce_scatter(blocks):
    n = blocks.shape[0]
    bits = n.bit_length() - 1
    return pl.pallas_call(
        functools.partial(reduce_kernel, bits),
        out_shape=jax.ShapeDtypeStruct(blocks.shape[1:], F32),
        in_specs=[VMEM_SPEC],
        out_specs=VMEM_SPEC,
        scratch_shapes=[
            pltpu.VMEM(blocks.shape, F32),
            pltpu.VMEM(blocks.shape, F32),
            pltpu.SemaphoreType.DMA((n, 2)),
            pltpu.SemaphoreType.DMA((n, 2)),
        ],
        compiler_params=pltpu.CompilerParams(collective_id=0, has_side_effects=True, vmem_limit_bytes=VMEM_LIMIT),
    )(blocks)


def misfit_kernel(count_ref, grid_ref, obs_ref, bins_ref, out_ref, lhs, acc):
    slots = bins_ref.shape[-1]
    parts, _, rows, _ = out_ref.shape
    for p in range(2):
        high, low = split(grid_ref[p].T)
        lhs[p * XM:(p + 1) * XM, :XM] = high
        lhs[p * XM:(p + 1) * XM, XM:] = low
    acc[...] = jnp.zeros_like(acc)
    count = count_ref[0, 0]
    chunk = 512

    @pl.loop(0, slots // chunk)
    def _(k):
        here = pl.ds(pl.multiple_of(k * chunk, chunk), chunk)
        bins = bins_ref[0, :, here]
        cell = iota((XM, chunk), 0)
        hot_u = jnp.where(cell == (bins >> 7), 1.0, 0.0).astype(BF16)
        at_v = cell == (bins & (XM - 1))
        picked = jnp.dot(lhs[...], jnp.concatenate([hot_u, hot_u], axis=0), preferred_element_type=F32)
        live = k * chunk + iota((1, chunk), 1) < count
        sides = []
        for p in range(2):
            predicted = jnp.sum(jnp.where(at_v, picked[p * XM:(p + 1) * XM], 0.0), axis=0, keepdims=True)
            misfit = jnp.where(live, obs_ref[0, 0, p:p + 1, here] - predicted, 0.0)
            high = misfit.astype(BF16).astype(F32)
            low = misfit - high
            sides.append(jnp.where(at_v, high, 0.0).astype(BF16))
            sides.append(jnp.where(at_v, low, 0.0).astype(BF16))
        acc[...] += lax.dot_general(
            hot_u, jnp.concatenate(sides, axis=0), (((1,), (1,)), ((), ())), preferred_element_type=F32
        )

    for p in range(2):
        value = acc[:, 2 * p * XM:(2 * p + 1) * XM] + acc[:, (2 * p + 1) * XM:(2 * p + 2) * XM]
        for q in range(parts):
            out_ref[q, p] = value[q * rows:(q + 1) * rows]


def misfits(parts, counts, grid, observed, bins):
    return pl.pallas_call(
        misfit_kernel,
        out_shape=jax.ShapeDtypeStruct((parts, 2, XM // parts, XM), F32),
        in_specs=[SMEM_SPEC] + [VMEM_SPEC] * 3,
        out_specs=VMEM_SPEC,
        scratch_shapes=[pltpu.VMEM((2 * XM, 2 * XM), BF16), pltpu.VMEM((XM, 4 * XM), F32)],
        compiler_params=pltpu.CompilerParams(vmem_limit_bytes=VMEM_LIMIT),
    )(counts, grid, observed, bins)


def gather_kernel(bits, parts, in_ref, off_ref, out_ref, zrecv, offs, zs, zr, os, orr, ts, tr, fs_sem, fr_sem):
    me = lax.axis_index("facet")
    mz = lax.axis_index("chan")
    barrier = pltpu.get_barrier_semaphore()
    for b in range(bits):
        pl.semaphore_signal(barrier, inc=1, device_id={"facet": flipped(me, b)}, device_id_type=MESH)
    for d in range(1, parts):
        pl.semaphore_signal(barrier, inc=1, device_id={"chan": (mz + d) % parts}, device_id_type=MESH)
    pl.semaphore_wait(barrier, bits + parts - 1)

    waits = []

    def chan_copy(src, dst, send, recv, d):
        copy = pltpu.make_async_remote_copy(
            src_ref=src, dst_ref=dst, send_sem=send.at[d - 1], recv_sem=recv.at[d - 1],
            device_id={"chan": (mz + d) % parts}, device_id_type=MESH,
        )
        copy.start()
        waits.append(copy)
        return copy

    small = [chan_copy(off_ref, offs.at[d - 1], os, orr, d) for d in range(1, parts)]
    first = [chan_copy(in_ref.at[(mz + d) % parts], zrecv.at[d - 1], zs, zr, d) for d in range(1, parts)]
    plain = in_ref[mz]
    scaled = off_ref[:1, :] * plain
    for d in range(1, parts):
        small[d - 1].wait_recv()
        first[d - 1].wait_recv()
        block = zrecv[d - 1]
        plain += block
        scaled += offs[d - 1, :1, :] * block
    out_ref[0, 0, 0] = plain
    out_ref[0, 0, 1] = scaled

    orders = [list(range(1, bits)) + [0], list(range(bits - 1, 0, -1)) + [0]]
    copies = {}

    def spread(d, j, r, start):
        for i in range(start, bits):
            bit = orders[j][i]
            to = r | (1 << bit)
            copy = pltpu.make_async_remote_copy(
                src_ref=out_ref.at[r, d, j], dst_ref=out_ref.at[to, d, j],
                send_sem=fs_sem.at[d, j, to], recv_sem=fr_sem.at[d, j, to],
                device_id={"facet": flipped(me, bit)}, device_id_type=MESH,
            )
            copy.start()
            copies[d, j, to] = copy
            waits.append(copy)

    second = [chan_copy(out_ref.at[0, 0], out_ref.at[0, d], ts, tr, d) for d in range(1, parts)]
    for j in range(2):
        spread(0, j, 0, 0)
    for tau in range(1, parts + bits + 1):
        if tau < parts:
            second[tau - 1].wait_recv()
            for j in range(2):
                spread(tau, j, 0, 0)
        for i in range(bits):
            d = tau - 1 - i
            if not 0 <= d < parts:
                continue
            for k in range(1 << i):
                for j in range(2):
                    held = sum(1 << orders[j][e] for e in range(i) if (k >> e) & 1)
                    r = held | (1 << orders[j][i])
                    copies[d, j, r].wait_recv()
                    spread(d, j, r, i + 1)
    for copy in waits:
        copy.wait_send()


def gather(facets, parts, blocks, offset_tile):
    bits = facets.bit_length() - 1
    rows = XM // parts
    dma = pltpu.SemaphoreType.DMA
    return pl.pallas_call(
        functools.partial(gather_kernel, bits, parts),
        out_shape=jax.ShapeDtypeStruct((facets, parts, 2, 2, rows, XM), F32),
        in_specs=[VMEM_SPEC] * 2,
        out_specs=VMEM_SPEC,
        scratch_shapes=[
            pltpu.VMEM((parts - 1, 2, rows, XM), F32),
            pltpu.VMEM((parts - 1,) + offset_tile.shape, F32),
        ] + [dma((parts - 1,))] * 6 + [dma((parts, 2, facets))] * 2,
        compiler_params=pltpu.CompilerParams(collective_id=1, has_side_effects=True, vmem_limit_bytes=VMEM_LIMIT),
    )(blocks, offset_tile)


def adjoint_kernel(rel_ref, pos_ref, in_ref, out_ref, bh, bl, ah, al, rh, rl, wh, wl):
    subs, parts, _, _, rows, _ = in_ref.shape
    share, fs = out_ref.shape[3:]
    cells = SUB_COLS * XM
    total = subs // SUB_COLS * XM
    row_pix, col_pix, mz = pos_ref[0] * fs, pos_ref[1] * fs, pos_ref[2]
    chunk = 64

    @pl.loop(0, cells // chunk)
    def _(k):
        base = pl.multiple_of(k * chunk, chunk)
        re, im = phases(base + iota((chunk, fs), 0), col_pix + iota((chunk, fs), 1))
        w = window(iota((8, fs), 1), fs)[:1]
        re, im = re * w, im * w
        top, low = pl.ds(base, chunk), pl.ds(pl.multiple_of(cells + base, chunk), chunk)
        put(bh, bl, (top, slice(0, fs)), re)
        put(bh, bl, (top, slice(fs, 2 * fs)), -im)
        put(bh, bl, (low, slice(0, fs)), im)
        put(bh, bl, (low, slice(fs, 2 * fs)), re)

    x = mz * share + iota((share, total), 0)
    re, im = phases(iota((share, total), 1), row_pix + x)
    w = window(mz * share + iota((share, XM), 0), fs)[:, :1]
    put(ah, al, (slice(None), slice(0, total)), re * w)
    put(ah, al, (slice(None), slice(total, 2 * total)), im * w)

    for s in range(subs):
        a, b = s // SUB_COLS, s % SUB_COLS
        slot = rel_ref[s]
        for d in range(parts):
            q = lax.rem(mz - d + parts, parts)
            top = pl.ds(pl.multiple_of(a * XM + q * rows, rows), rows)
            low = pl.ds(pl.multiple_of(total + a * XM + q * rows, rows), rows)
            for j in range(2):
                left = slice(2 * j * cells + b * XM, 2 * j * cells + (b + 1) * XM)
                right = slice((2 * j + 1) * cells + b * XM, (2 * j + 1) * cells + (b + 1) * XM)
                high, small = split(in_ref[slot, d, j, 0])
                rh[top, left] = high
                rl[top, left] = small
                rh[low, right] = -high
                rl[low, right] = -small
                high, small = split(in_ref[slot, d, j, 1])
                rh[top, right] = high
                rl[top, right] = small
                rh[low, left] = high
                rl[low, left] = small

    tile = 256
    for k in range(4 * cells // tile):
        cols = slice(k * tile, (k + 1) * tile)
        part = dot3(ah[...], al[...], rh[:, cols], rl[:, cols])
        j, rest = k * tile // (2 * cells), k * tile % (2 * cells)
        put(wh, wl, (slice(j * share, (j + 1) * share), slice(rest, rest + tile)), part)
    for k in range(2 * fs // tile):
        cols = slice(k * tile, (k + 1) * tile)
        part = dot3(wh[...], wl[...], bh[:, cols], bl[:, cols])
        p, rest = k * tile // fs, k * tile % fs
        for j in range(2):
            out_ref[j, 0, p, :, rest:rest + tile] = part[j * share:(j + 1) * share]


def adjoint(rel, pos, gathered, share, fs):
    subs = gathered.shape[0]
    cells = SUB_COLS * XM
    total = subs // SUB_COLS * XM
    return pl.pallas_call(
        adjoint_kernel,
        out_shape=jax.ShapeDtypeStruct((2, 1, 2, share, fs), F32),
        in_specs=[SMEM_SPEC] * 2 + [VMEM_SPEC],
        out_specs=VMEM_SPEC,
        scratch_shapes=[
            pltpu.VMEM((2 * cells, 2 * fs), BF16),
            pltpu.VMEM((2 * cells, 2 * fs), BF16),
            pltpu.VMEM((share, 2 * total), BF16),
            pltpu.VMEM((share, 2 * total), BF16),
            pltpu.VMEM((2 * total, 4 * cells), BF16),
            pltpu.VMEM((2 * total, 4 * cells), BF16),
            pltpu.VMEM((2 * share, 2 * cells), BF16),
            pltpu.VMEM((2 * share, 2 * cells), BF16),
        ],
        compiler_params=pltpu.CompilerParams(vmem_limit_bytes=VMEM_LIMIT),
    )(rel, pos, gathered)


def solution(mesh):
    facets, parts = mesh.shape["facet"], mesh.shape["chan"]

    def on_device(model_taylor, channel_offset, assignment, observed, uv_bins, vis_counts):
        me, mz = lax.axis_index("facet"), lax.axis_index("chan")
        subs, fs = assignment.shape[0], model_taylor.shape[-1]
        numbers = jnp.arange(subs, dtype=jnp.int32)
        rel = jnp.sum(jnp.where(assignment[None, :] == numbers[:, None], numbers[None, :] ^ me, 0), axis=1)
        pos = jnp.stack([me // FACET_COLS, me % FACET_COLS, mz]).astype(jnp.int32)
        blocks = predict(subs, rel, pos, channel_offset, model_taylor)
        grid = reduce_scatter(blocks)
        spread = misfits(parts, vis_counts, grid, observed, uv_bins)
        gathered = gather(facets, parts, spread, jnp.broadcast_to(channel_offset, (8, XM)))
        return adjoint(rel, pos, gathered, fs // parts, fs)

    return jax.shard_map(
        on_device,
        mesh=mesh,
        in_specs=(
            P(None, "facet", None, None, None),
            P("chan"),
            P(),
            P("chan", "facet", None, None),
            P("chan", "facet", None),
            P("chan", "facet"),
        ),
        out_specs=P(None, "facet", None, "chan", None),
        check_vma=False,
    )
```

```python
import functools

import jax
import jax.numpy as jnp
from jax import lax
from jax.experimental import pallas as pl
from jax.experimental.pallas import tpu as pltpu
from jax.sharding import PartitionSpec as P

XM = 128
FACET_COLS = 4
SUB_COLS = 4
IMAGE = 2048
TWO_PI = 6.283185307179586
F32 = jnp.float32
BF16 = jnp.bfloat16
MESH = pl.DeviceIdType.MESH
VMEM_SPEC = pl.BlockSpec(memory_space=pltpu.VMEM)
SMEM_SPEC = pl.BlockSpec(memory_space=pltpu.SMEM)
VMEM_LIMIT = 56 * 1024 * 1024


def cos_sin(turns):
    quarter = IMAGE // 4
    shift = quarter.bit_length() - 1
    step = (turns + quarter // 2) >> shift
    rest = turns - (step << shift)
    t = rest.astype(F32) * (TWO_PI / IMAGE)
    t2 = t * t
    s = t * (1.0 + t2 * (-1.0 / 6 + t2 * (1.0 / 120 + t2 * (-1.0 / 5040 + t2 * (1.0 / 362880)))))
    c = 1.0 + t2 * (-0.5 + t2 * (1.0 / 24 + t2 * (-1.0 / 720 + t2 * (1.0 / 40320))))
    odd = (step & 1) == 1
    cos = jnp.where(odd, s, c)
    sin = jnp.where(odd, c, s)
    cos = jnp.where(((step + 1) & 2) == 2, -cos, cos)
    sin = jnp.where((step & 2) == 2, -sin, sin)
    return cos, sin


def window(positions, length):
    cos, _ = cos_sin(((2 * positions + 1 - length) * (IMAGE // (2 * length))) & (IMAGE - 1))
    return (0.55 + 0.45 * cos) * (float(length) ** -0.5)


def phases(frequency, pixel):
    cos, sin = cos_sin((frequency * pixel) & (IMAGE - 1))
    return cos, -sin


def split(value):
    high = value.astype(BF16)
    return high, (value - high.astype(F32)).astype(BF16)


def put(high_ref, low_ref, where, value):
    high, low = split(value)
    high_ref[where] = high
    low_ref[where] = low


def dot3(a_high, a_low, b_high, b_low):
    dot = functools.partial(jnp.dot, preferred_element_type=F32)
    return dot(a_high, b_high) + (dot(a_low, b_high) + dot(a_high, b_low))


def iota(shape, dim):
    return lax.broadcasted_iota(jnp.int32, shape, dim)


def flipped(me, bit):
    size = 1 << bit
    return me + (1 - 2 * ((me // size) % 2)) * size


def flipped_all(me, mask):
    for bit in range(mask.bit_length()):
        if (mask >> bit) & 1:
            me = flipped(me, bit)
    return me


def build_forward(fs, row_pix, col_pix, halves, bh, bl, ah, al):
    cells = bh.shape[1] // 2
    total = ah.shape[0]
    chunk = 64

    @pl.loop(0, fs // chunk)
    def _(k):
        base = pl.multiple_of(k * chunk, chunk)
        y = base + iota((chunk, cells), 0)
        re, im = phases(iota((chunk, cells), 1), col_pix + y)
        w = window(base + iota((chunk, XM), 0), fs)[:, :1]
        re, im = re * w, im * w
        top, low = pl.ds(base, chunk), pl.ds(pl.multiple_of(fs + base, chunk), chunk)
        put(bh, bl, (top, slice(0, cells)), re)
        put(bh, bl, (top, slice(cells, 2 * cells)), im)
        put(bh, bl, (low, slice(0, cells)), -im)
        put(bh, bl, (low, slice(cells, 2 * cells)), re)

    @pl.loop(0, total // chunk)
    def _(k):
        base = pl.multiple_of(k * chunk, chunk)
        x = iota((chunk, fs), 1)
        re, im = phases(base + iota((chunk, fs), 0), row_pix + x)
        w = window(iota((8, fs), 1), fs)[:1]
        rows = pl.ds(base, chunk)
        put(ah, al, (rows, slice(0, fs)), re * w)
        put(ah, al, (rows, slice(fs, 2 * fs)), im * w)


def build_adjoint(fs, share, row_pix, col_pix, mz, bh, bl, ah, al):
    cells = bh.shape[0] // 2
    total = ah.shape[1] // 2
    chunk = 64

    @pl.loop(0, cells // chunk)
    def _(k):
        base = pl.multiple_of(k * chunk, chunk)
        re, im = phases(base + iota((chunk, fs), 0), col_pix + iota((chunk, fs), 1))
        w = window(iota((8, fs), 1), fs)[:1]
        re, im = re * w, im * w
        top, low = pl.ds(base, chunk), pl.ds(pl.multiple_of(cells + base, chunk), chunk)
        put(bh, bl, (top, slice(0, fs)), re)
        put(bh, bl, (top, slice(fs, 2 * fs)), -im)
        put(bh, bl, (low, slice(0, fs)), im)
        put(bh, bl, (low, slice(fs, 2 * fs)), re)

    x = mz * share + iota((share, total), 0)
    re, im = phases(iota((share, total), 1), row_pix + x)
    w = window(mz * share + iota((share, XM), 0), fs)[:, :1]
    put(ah, al, (slice(None), slice(0, total)), re * w)
    put(ah, al, (slice(None), slice(total, 2 * total)), im * w)


def image_rows(i, offset, fs, xb, mbuf, mh, ml, bh, bl, ph, plo):
    cells = bh.shape[1] // 2
    for p in range(2):
        value = mbuf[i, 0, p] + offset * mbuf[i, 1, p]
        put(mh, ml, (slice(None), slice(p * fs, (p + 1) * fs)), value)
    tile = 256
    top, low = slice(i * xb, (i + 1) * xb), slice(fs + i * xb, fs + (i + 1) * xb)
    for k in range(2 * cells // tile):
        cols = slice(k * tile, (k + 1) * tile)
        part = dot3(mh[...], ml[...], bh[:, cols], bl[:, cols])
        high, small = split(part)
        ph[top, cols] = high
        plo[top, cols] = small
        if k * tile < cells:
            other = slice(k * tile + cells, (k + 1) * tile + cells)
        else:
            other = slice(k * tile - cells, (k + 1) * tile - cells)
            high, small = -high, -small
        ph[low, other] = high
        plo[low, other] = small


def subgrid_plane(p, subs, ah, al, ph, plo, out):
    cells = ph.shape[1] // 2
    tile = 256
    for k in range(cells // tile):
        part = dot3(
            ah[...], al[...],
            ph[:, p * cells + k * tile:p * cells + (k + 1) * tile],
            plo[:, p * cells + k * tile:p * cells + (k + 1) * tile],
        )
        for a in range(subs // SUB_COLS):
            for b in range(tile // XM):
                s = a * SUB_COLS + k * (tile // XM) + b
                out[s, p] = part[a * XM:(a + 1) * XM, b * XM:(b + 1) * XM]


def misfit_blocks(count_ref, grid_ref, obs_ref, bins_ref, out_ref, lhs, acc):
    slots = bins_ref.shape[-1]
    parts, _, rows, _ = out_ref.shape
    for p in range(2):
        high, low = split(grid_ref[p].T)
        lhs[p * XM:(p + 1) * XM, :XM] = high
        lhs[p * XM:(p + 1) * XM, XM:] = low
    acc[...] = jnp.zeros_like(acc)
    count = count_ref[0, 0]
    chunk = 512

    @pl.loop(0, slots // chunk)
    def _(k):
        here = pl.ds(pl.multiple_of(k * chunk, chunk), chunk)
        bins = bins_ref[0, :, here]
        cell = iota((XM, chunk), 0)
        hot_u = jnp.where(cell == (bins >> 7), 1.0, 0.0).astype(BF16)
        at_v = cell == (bins & (XM - 1))
        picked = jnp.dot(lhs[...], jnp.concatenate([hot_u, hot_u], axis=0), preferred_element_type=F32)
        live = k * chunk + iota((1, chunk), 1) < count
        hot_v = jnp.where(at_v, 1.0, 0.0).astype(BF16)
        sides = []
        for p in range(2):
            predicted = jnp.sum(jnp.where(at_v, picked[p * XM:(p + 1) * XM], 0.0), axis=0, keepdims=True)
            misfit = jnp.where(live, obs_ref[0, 0, p:p + 1, here] - predicted, 0.0)
            high, low = split(misfit)
            sides.append(hot_v * high)
            sides.append(hot_v * low)
        acc[...] += lax.dot_general(
            hot_u, jnp.concatenate(sides, axis=0), (((1,), (1,)), ((), ())), preferred_element_type=F32
        )

    for p in range(2):
        value = acc[:, 2 * p * XM:(2 * p + 1) * XM] + acc[:, (2 * p + 1) * XM:(2 * p + 2) * XM]
        for q in range(parts):
            out_ref[q, p] = value[q * rows:(q + 1) * rows]


def adjoint_rows(subs, parts, slots, mz, in_ref, rh, rl):
    rows = in_ref.shape[-2]
    cells = SUB_COLS * XM
    total = rh.shape[0] // 2
    for s in range(subs):
        a, b = s // SUB_COLS, s % SUB_COLS
        for d in range(parts):
            q = (mz - d + parts) % parts
            top = pl.ds(pl.multiple_of(a * XM + q * rows, rows), rows)
            low = pl.ds(pl.multiple_of(total + a * XM + q * rows, rows), rows)
            for j in range(2):
                left = slice(2 * j * cells + b * XM, 2 * j * cells + (b + 1) * XM)
                right = slice((2 * j + 1) * cells + b * XM, (2 * j + 1) * cells + (b + 1) * XM)
                high, small = split(in_ref[slots[s], d, j, 0])
                rh[top, left] = high
                rl[top, left] = small
                rh[low, right] = -high
                rl[low, right] = -small
                high, small = split(in_ref[slots[s], d, j, 1])
                rh[top, right] = high
                rl[top, right] = small
                rh[low, left] = high
                rl[low, left] = small


def adjoint_images(share, fs, out_ref, bh, bl, ah, al, rh, rl, wh, wl):
    cells = SUB_COLS * XM
    tile = 256
    for k in range(4 * cells // tile):
        cols = slice(k * tile, (k + 1) * tile)
        part = dot3(ah[...], al[...], rh[:, cols], rl[:, cols])
        j, rest = k * tile // (2 * cells), k * tile % (2 * cells)
        put(wh, wl, (slice(j * share, (j + 1) * share), slice(rest, rest + tile)), part)
    for k in range(2 * fs // tile):
        cols = slice(k * tile, (k + 1) * tile)
        part = dot3(wh[...], wl[...], bh[:, cols], bl[:, cols])
        p, rest = k * tile // fs, k * tile % fs
        for j in range(2):
            out_ref[j, 0, p, :, rest:rest + tile] = part[j * share:(j + 1) * share]


def cycle_kernel(
    names, bits, parts, assign_ref, off_ref, count_ref, model_ref, obs_ref, bins_ref, out_ref, *scratch
):
    m = dict(zip(names, scratch))
    me, mz = lax.axis_index("facet"), lax.axis_index("chan")
    subs, fs, share = assign_ref.shape[0], model_ref.shape[-1], out_ref.shape[3]
    halves, xb = m["mbuf"].shape[0], m["mbuf"].shape[3]
    row_pix, col_pix = (me // FACET_COLS) * fs, (me % FACET_COLS) * fs

    loads = []
    for i in range(halves):
        load = pltpu.make_async_copy(
            model_ref.at[:, 0, :, pl.ds(i * xb, xb), :], m["mbuf"].at[i], m["load_sem"].at[i]
        )
        load.start()
        loads.append(load)
    barrier = pltpu.get_barrier_semaphore()
    for b in range(bits):
        pl.semaphore_signal(barrier, inc=1, device_id={"facet": flipped(me, b)}, device_id_type=MESH)
    for d in range(1, parts):
        pl.semaphore_signal(barrier, inc=1, device_id={"chan": (mz + d) % parts}, device_id_type=MESH)

    offset = off_ref[0]
    m["tile"][...] = jnp.full(m["tile"].shape, offset, F32)
    build_forward(fs, row_pix, col_pix, halves, m["bh"], m["bl"], m["ah"], m["al"])
    subgrid_of = [assign_ref[flipped_all(me, r)] for r in range(subs)]
    slots = []
    for s in range(subs):
        slot = jnp.int32(0)
        for r in range(1, subs):
            slot = jnp.where(subgrid_of[r] == s, r, slot)
        slots.append(slot)
    for i in range(halves):
        loads[i].wait()
        image_rows(i, offset, fs, xb, m["mbuf"], m["mh"], m["ml"], m["bh"], m["bl"], m["ph"], m["plo"])

    waits = []

    def chan_copy(src, dst, send, recv, d):
        copy = pltpu.make_async_remote_copy(
            src_ref=src, dst_ref=dst, send_sem=send.at[d - 1], recv_sem=recv.at[d - 1],
            device_id={"chan": (mz + d) % parts}, device_id_type=MESH,
        )
        copy.start()
        waits.append(copy)
        return copy

    orders = [[0] + list(range(1, bits)), [0] + list(range(bits - 1, 0, -1))]
    blk, acc, recv = m["blk"], m["acc"], m["recv"]
    source = {(r, p): blk for r in range(1 << bits) for p in range(2)}
    copies = {}

    def send(r, p, bit):
        copy = pltpu.make_async_remote_copy(
            src_ref=source[r, p].at[r, p],
            dst_ref=recv.at[r, p],
            send_sem=m["rs_send"].at[r, p],
            recv_sem=m["rs_recv"].at[r, p],
            device_id={"facet": flipped(me, bit)},
            device_id_type=MESH,
        )
        copy.start()
        copies[r, p] = copy
        waits.append(copy)

    def ranked(members, later):
        return sorted(members, key=lambda r: [-((r >> b) & 1) for b in later])

    for p in range(2):
        subgrid_plane(p, subs, m["ah"], m["al"], m["ph"], m["plo"], m["grids"])
        for r in range(subs):
            blk[r, p] = m["grids"][subgrid_of[r], p]
        if p == 0:
            pl.semaphore_wait(barrier, bits + parts - 1)
        for r in ranked([r for r in range(subs) if (r >> orders[p][0]) & 1], orders[p][1:]):
            send(r, p, orders[p][0])
    small = [chan_copy(m["tile"], m["offs"].at[d - 1], m["off_send"], m["off_recv"], d) for d in range(1, parts)]

    build_adjoint(fs, share, row_pix, col_pix, mz, m["cbh"], m["cbl"], m["cah"], m["cal"])

    members = [list(range(1 << bits)) for _ in range(2)]
    for i in range(bits):
        kept = []
        for p in range(2):
            bit = orders[p][i]
            members[p] = ranked([r for r in members[p] if not (r >> bit) & 1], orders[p][i + 1:])
            kept.append(members[p])
        for pair in zip(*kept):
            for p in range(2):
                r, bit = pair[p], orders[p][i]
                copies[r | (1 << bit), p].wait_recv()
                acc[r, p] = source[r, p][r, p] + recv[r | (1 << bit), p]
                source[r, p] = acc
                if i < bits - 1 and (r >> orders[p][i + 1]) & 1:
                    send(r, p, orders[p][i + 1])

    zsend, zrecv, offs, gbuf = m["zsend"], m["zrecv"], m["offs"], m["gbuf"]
    misfit_blocks(count_ref, acc.at[0], obs_ref, bins_ref, zsend, m["lhs"], m["macc"])

    first = [chan_copy(zsend.at[(mz + d) % parts], zrecv.at[d - 1], m["z_send"], m["z_recv"], d) for d in range(1, parts)]
    plain = zsend[mz]
    scaled = offset * plain
    for d in range(1, parts):
        small[d - 1].wait_recv()
        first[d - 1].wait_recv()
        block = zrecv[d - 1]
        plain += block
        scaled += offs[d - 1, :1, :] * block
    gbuf[0, 0, 0] = plain
    gbuf[0, 0, 1] = scaled

    spread_orders = [list(range(1, bits)) + [0], list(range(bits - 1, 0, -1)) + [0]]
    landed = {}

    def spread(d, j, r, start):
        for i in range(start, bits):
            bit = spread_orders[j][i]
            to = r | (1 << bit)
            copy = pltpu.make_async_remote_copy(
                src_ref=gbuf.at[r, d, j], dst_ref=gbuf.at[to, d, j],
                send_sem=m["ag_send"].at[d, j, to], recv_sem=m["ag_recv"].at[d, j, to],
                device_id={"facet": flipped(me, bit)}, device_id_type=MESH,
            )
            copy.start()
            landed[d, j, to] = copy
            waits.append(copy)

    second = [chan_copy(gbuf.at[0, 0], gbuf.at[0, d], m["t_send"], m["t_recv"], d) for d in range(1, parts)]
    for j in range(2):
        spread(0, j, 0, 0)
    for tau in range(1, parts + bits + 1):
        if tau < parts:
            second[tau - 1].wait_recv()
            for j in range(2):
                spread(tau, j, 0, 0)
        for i in range(bits):
            d = tau - 1 - i
            if not 0 <= d < parts:
                continue
            for k in range(1 << i):
                for j in range(2):
                    held = sum(1 << spread_orders[j][e] for e in range(i) if (k >> e) & 1)
                    r = held | (1 << spread_orders[j][i])
                    landed[d, j, r].wait_recv()
                    spread(d, j, r, i + 1)
    adjoint_rows(subs, parts, slots, mz, gbuf, m["rh"], m["rl"])
    adjoint_images(
        share, fs, out_ref, m["cbh"], m["cbl"], m["cah"], m["cal"], m["rh"], m["rl"], m["wh"], m["wl"]
    )
    for copy in waits:
        copy.wait_send()


def solution(mesh):
    facets, parts = mesh.shape["facet"], mesh.shape["chan"]
    bits = facets.bit_length() - 1

    def on_device(model_taylor, channel_offset, assignment, observed, uv_bins, vis_counts):
        subs, fs = assignment.shape[0], model_taylor.shape[-1]
        share, rows, halves = fs // parts, XM // parts, 2
        xb = fs // halves
        cells, total = SUB_COLS * XM, subs // SUB_COLS * XM
        vmem, dma = pltpu.VMEM, pltpu.SemaphoreType.DMA
        scratch = {
            "mbuf": vmem((halves, 2, 2, xb, fs), F32),
            "tile": vmem((8, XM), F32),
            "offs": vmem((parts - 1, 8, XM), F32),
            "grids": vmem((subs, 2, XM, XM), F32),
            "blk": vmem((subs, 2, XM, XM), F32),
            "acc": vmem((subs, 2, XM, XM), F32),
            "recv": vmem((subs, 2, XM, XM), F32),
            "lhs": vmem((2 * XM, 2 * XM), BF16),
            "macc": vmem((XM, 4 * XM), F32),
            "zsend": vmem((parts, 2, rows, XM), F32),
            "zrecv": vmem((parts - 1, 2, rows, XM), F32),
            "gbuf": vmem((facets, parts, 2, 2, rows, XM), F32),
        }
        for high, low, shape in (
            ("bh", "bl", (2 * fs, 2 * cells)),
            ("ah", "al", (total, 2 * fs)),
            ("mh", "ml", (xb, 2 * fs)),
            ("ph", "plo", (2 * fs, 2 * cells)),
            ("cbh", "cbl", (2 * cells, 2 * fs)),
            ("cah", "cal", (share, 2 * total)),
            ("rh", "rl", (2 * total, 4 * cells)),
            ("wh", "wl", (2 * share, 2 * cells)),
        ):
            scratch[high] = vmem(shape, BF16)
            scratch[low] = vmem(shape, BF16)
        scratch["load_sem"] = dma((halves,))
        scratch["rs_send"] = scratch["rs_recv"] = dma((facets, 2))
        for name in ("off", "z", "t"):
            scratch[name + "_send"] = scratch[name + "_recv"] = dma((parts - 1,))
        scratch["ag_send"] = scratch["ag_recv"] = dma((parts, 2, facets))
        return pl.pallas_call(
            functools.partial(cycle_kernel, list(scratch), bits, parts),
            out_shape=jax.ShapeDtypeStruct((2, 1, 2, share, fs), F32),
            in_specs=[SMEM_SPEC] * 3 + [pl.BlockSpec(memory_space=pl.ANY)] + [VMEM_SPEC] * 2,
            out_specs=VMEM_SPEC,
            scratch_shapes=list(scratch.values()),
            compiler_params=pltpu.CompilerParams(
                collective_id=0, has_side_effects=True, vmem_limit_bytes=VMEM_LIMIT
            ),
        )(assignment, channel_offset, vis_counts, model_taylor, observed, uv_bins)

    return jax.shard_map(
        on_device,
        mesh=mesh,
        in_specs=(
            P(None, "facet", None, None, None),
            P("chan"),
            P(),
            P("chan", "facet", None, None),
            P("chan", "facet", None),
            P("chan", "facet"),
        ),
        out_specs=P(None, "facet", None, "chan", None),
        check_vma=False,
    )
```

```python
import functools

import jax
import jax.numpy as jnp
from jax import lax
from jax.experimental import pallas as pl
from jax.experimental.pallas import tpu as pltpu
from jax.sharding import PartitionSpec as P

XM = 128
FACET_COLS = 4
SUB_COLS = 4
IMAGE = 2048
TWO_PI = 6.283185307179586
F32 = jnp.float32
BF16 = jnp.bfloat16
MESH = pl.DeviceIdType.MESH
VMEM_SPEC = pl.BlockSpec(memory_space=pltpu.VMEM)
SMEM_SPEC = pl.BlockSpec(memory_space=pltpu.SMEM)
VMEM_LIMIT = 56 * 1024 * 1024


def cos_sin(turns):
    quarter = IMAGE // 4
    shift = quarter.bit_length() - 1
    step = (turns + quarter // 2) >> shift
    rest = turns - (step << shift)
    t = rest.astype(F32) * (TWO_PI / IMAGE)
    t2 = t * t
    s = t * (1.0 + t2 * (-1.0 / 6 + t2 * (1.0 / 120 + t2 * (-1.0 / 5040 + t2 * (1.0 / 362880)))))
    c = 1.0 + t2 * (-0.5 + t2 * (1.0 / 24 + t2 * (-1.0 / 720 + t2 * (1.0 / 40320))))
    odd = (step & 1) == 1
    cos = jnp.where(odd, s, c)
    sin = jnp.where(odd, c, s)
    cos = jnp.where(((step + 1) & 2) == 2, -cos, cos)
    sin = jnp.where((step & 2) == 2, -sin, sin)
    return cos, sin


def window(positions, length):
    cos, _ = cos_sin(((2 * positions + 1 - length) * (IMAGE // (2 * length))) & (IMAGE - 1))
    return (0.55 + 0.45 * cos) * (float(length) ** -0.5)


def phases(frequency, pixel):
    cos, sin = cos_sin((frequency * pixel) & (IMAGE - 1))
    return cos, -sin


def split(value):
    high = value.astype(BF16)
    return high, (value - high.astype(F32)).astype(BF16)


def put(high_ref, low_ref, where, value):
    high, low = split(value)
    high_ref[where] = high
    low_ref[where] = low


def dot3(a_high, a_low, b_high, b_low):
    dot = functools.partial(jnp.dot, preferred_element_type=F32)
    return dot(a_high, b_high) + (dot(a_low, b_high) + dot(a_high, b_low))


def iota(shape, dim):
    return lax.broadcasted_iota(jnp.int32, shape, dim)


def flipped(me, bit):
    size = 1 << bit
    return me + (1 - 2 * ((me // size) % 2)) * size


def flipped_all(me, mask):
    for bit in range(mask.bit_length()):
        if (mask >> bit) & 1:
            me = flipped(me, bit)
    return me


def build_forward(fs, row_pix, col_pix, halves, bh, bl, ah, al):
    cells = bh.shape[1] // 2
    total = ah.shape[0]
    chunk = 64

    @pl.loop(0, fs // chunk)
    def _(k):
        base = pl.multiple_of(k * chunk, chunk)
        y = base + iota((chunk, cells), 0)
        re, im = phases(iota((chunk, cells), 1), col_pix + y)
        w = window(base + iota((chunk, XM), 0), fs)[:, :1]
        re, im = re * w, im * w
        top, low = pl.ds(base, chunk), pl.ds(pl.multiple_of(fs + base, chunk), chunk)
        put(bh, bl, (top, slice(0, cells)), re)
        put(bh, bl, (top, slice(cells, 2 * cells)), im)
        put(bh, bl, (low, slice(0, cells)), -im)
        put(bh, bl, (low, slice(cells, 2 * cells)), re)

    @pl.loop(0, total // chunk)
    def _(k):
        base = pl.multiple_of(k * chunk, chunk)
        x = iota((chunk, fs), 1)
        re, im = phases(base + iota((chunk, fs), 0), row_pix + x)
        w = window(iota((8, fs), 1), fs)[:1]
        rows = pl.ds(base, chunk)
        put(ah, al, (rows, slice(0, fs)), re * w)
        put(ah, al, (rows, slice(fs, 2 * fs)), im * w)


def build_adjoint(fs, share, row_pix, col_pix, mz, bh, bl, ah, al):
    cells = bh.shape[0] // 2
    total = ah.shape[1] // 2
    chunk = 64

    @pl.loop(0, cells // chunk)
    def _(k):
        base = pl.multiple_of(k * chunk, chunk)
        re, im = phases(base + iota((chunk, fs), 0), col_pix + iota((chunk, fs), 1))
        w = window(iota((8, fs), 1), fs)[:1]
        re, im = re * w, im * w
        top, low = pl.ds(base, chunk), pl.ds(pl.multiple_of(cells + base, chunk), chunk)
        put(bh, bl, (top, slice(0, fs)), re)
        put(bh, bl, (top, slice(fs, 2 * fs)), -im)
        put(bh, bl, (low, slice(0, fs)), im)
        put(bh, bl, (low, slice(fs, 2 * fs)), re)

    x = mz * share + iota((share, total), 0)
    re, im = phases(iota((share, total), 1), row_pix + x)
    w = window(mz * share + iota((share, XM), 0), fs)[:, :1]
    put(ah, al, (slice(None), slice(0, total)), re * w)
    put(ah, al, (slice(None), slice(total, 2 * total)), im * w)


def image_rows(i, offset, fs, xb, mbuf, mh, ml, bh, bl, ph, plo):
    cells = bh.shape[1] // 2
    for p in range(2):
        value = mbuf[i, 0, p] + offset * mbuf[i, 1, p]
        put(mh, ml, (slice(None), slice(p * fs, (p + 1) * fs)), value)
    tile = 256
    top, low = slice(i * xb, (i + 1) * xb), slice(fs + i * xb, fs + (i + 1) * xb)
    for k in range(2 * cells // tile):
        cols = slice(k * tile, (k + 1) * tile)
        part = dot3(mh[...], ml[...], bh[:, cols], bl[:, cols])
        high, small = split(part)
        ph[top, cols] = high
        plo[top, cols] = small
        if k * tile < cells:
            other = slice(k * tile + cells, (k + 1) * tile + cells)
        else:
            other = slice(k * tile - cells, (k + 1) * tile - cells)
            high, small = -high, -small
        ph[low, other] = high
        plo[low, other] = small


def subgrid_plane(p, subs, ah, al, ph, plo, out):
    cells = ph.shape[1] // 2
    tile = 256
    for k in range(cells // tile):
        part = dot3(
            ah[...], al[...],
            ph[:, p * cells + k * tile:p * cells + (k + 1) * tile],
            plo[:, p * cells + k * tile:p * cells + (k + 1) * tile],
        )
        for a in range(subs // SUB_COLS):
            for b in range(tile // XM):
                s = a * SUB_COLS + k * (tile // XM) + b
                out[s, p] = part[a * XM:(a + 1) * XM, b * XM:(b + 1) * XM]


def build_hot(bins_ref, hot_u, hot_v):
    slots = bins_ref.shape[-1]
    chunk = 512

    @pl.loop(0, slots // chunk)
    def _(k):
        here = pl.ds(pl.multiple_of(k * chunk, chunk), chunk)
        bins = bins_ref[0, :, here]
        cell = iota((XM, chunk), 0)
        at_u = jnp.where(cell == (bins >> 7), 1.0, 0.0).astype(BF16)
        hot_u[:XM, here] = at_u
        hot_u[XM:, here] = at_u
        hot_v[:, here] = jnp.where(cell == (bins & (XM - 1)), 1.0, 0.0).astype(BF16)


def misfit_blocks(count_ref, grid_ref, obs_ref, bins_ref, out_ref, lhs, hot_u, hot_v, sides):
    slots = bins_ref.shape[-1]
    parts, _, rows, _ = out_ref.shape
    for p in range(2):
        high, low = split(grid_ref[p].T)
        lhs[p * XM:(p + 1) * XM, :XM] = high
        lhs[p * XM:(p + 1) * XM, XM:] = low
    count = count_ref[0, 0]
    chunk = 512
    for k in range(slots // chunk):
        here = slice(k * chunk, (k + 1) * chunk)
        at_v = iota((XM, chunk), 0) == (bins_ref[0, :, here] & (XM - 1))
        picked = jnp.dot(lhs[...], hot_u[:, here], preferred_element_type=F32)
        live = k * chunk + iota((1, chunk), 1) < count
        ones = hot_v[:, here]
        for p in range(2):
            predicted = jnp.sum(jnp.where(at_v, picked[p * XM:(p + 1) * XM], 0.0), axis=0, keepdims=True)
            misfit = jnp.where(live, obs_ref[0, 0, p:p + 1, here] - predicted, 0.0)
            high, low = split(misfit)
            sides[2 * p * XM:(2 * p + 1) * XM, here] = ones * high
            sides[(2 * p + 1) * XM:(2 * p + 2) * XM, here] = ones * low

    for p in range(2):
        both = lax.dot_general(
            hot_u[:XM, :], sides[2 * p * XM:(2 * p + 2) * XM, :], (((1,), (1,)), ((), ())),
            preferred_element_type=F32,
        )
        value = both[:, :XM] + both[:, XM:]
        for q in range(parts):
            out_ref[q, p] = value[q * rows:(q + 1) * rows]


def adjoint_rows(subs, slots, q, in_ref, rh, rl):
    rows = in_ref.shape[-2]
    cells = SUB_COLS * XM
    total = rh.shape[0] // 2
    for s in range(subs):
        a, b = s // SUB_COLS, s % SUB_COLS
        top = pl.ds(pl.multiple_of(a * XM + q * rows, rows), rows)
        low = pl.ds(pl.multiple_of(total + a * XM + q * rows, rows), rows)
        for j in range(2):
            left = slice(2 * j * cells + b * XM, 2 * j * cells + (b + 1) * XM)
            right = slice((2 * j + 1) * cells + b * XM, (2 * j + 1) * cells + (b + 1) * XM)
            high, small = split(in_ref[slots[s], j, 0])
            rh[top, left] = high
            rl[top, left] = small
            rh[low, right] = -high
            rl[low, right] = -small
            high, small = split(in_ref[slots[s], j, 1])
            rh[top, right] = high
            rl[top, right] = small
            rh[low, left] = high
            rl[low, left] = small


def adjoint_images(share, fs, out_ref, bh, bl, ah, al, rh, rl, wh, wl):
    cells = SUB_COLS * XM
    tile = 256
    for k in range(4 * cells // tile):
        cols = slice(k * tile, (k + 1) * tile)
        part = dot3(ah[...], al[...], rh[:, cols], rl[:, cols])
        j, rest = k * tile // (2 * cells), k * tile % (2 * cells)
        put(wh, wl, (slice(j * share, (j + 1) * share), slice(rest, rest + tile)), part)
    for k in range(2 * fs // tile):
        cols = slice(k * tile, (k + 1) * tile)
        part = dot3(wh[...], wl[...], bh[:, cols], bl[:, cols])
        p, rest = k * tile // fs, k * tile % fs
        for j in range(2):
            out_ref[j, 0, p, :, rest:rest + tile] = part[j * share:(j + 1) * share]


def cycle_kernel(
    names, bits, parts, assign_ref, off_ref, count_ref, model_ref, obs_ref, bins_ref, out_ref, *scratch
):
    m = dict(zip(names, scratch))
    me, mz = lax.axis_index("facet"), lax.axis_index("chan")
    subs, fs, share = assign_ref.shape[0], model_ref.shape[-1], out_ref.shape[3]
    halves, xb = m["mbuf"].shape[0], m["mbuf"].shape[3]
    row_pix, col_pix = (me // FACET_COLS) * fs, (me % FACET_COLS) * fs

    loads = []
    for i in range(halves):
        load = pltpu.make_async_copy(
            model_ref.at[:, 0, :, pl.ds(i * xb, xb), :], m["mbuf"].at[i], m["load_sem"].at[i]
        )
        load.start()
        loads.append(load)
    barrier = pltpu.get_barrier_semaphore()
    for b in range(bits):
        pl.semaphore_signal(barrier, inc=1, device_id={"facet": flipped(me, b)}, device_id_type=MESH)
    for d in range(1, parts):
        pl.semaphore_signal(barrier, inc=1, device_id={"chan": flipped_all(mz, d)}, device_id_type=MESH)

    offset = off_ref[0]
    m["tile"][...] = jnp.full(m["tile"].shape, offset, F32)
    build_forward(fs, row_pix, col_pix, halves, m["bh"], m["bl"], m["ah"], m["al"])
    subgrid_of = [assign_ref[flipped_all(me, r)] for r in range(subs)]
    slots = []
    for s in range(subs):
        slot = jnp.int32(0)
        for r in range(1, subs):
            slot = jnp.where(subgrid_of[r] == s, r, slot)
        slots.append(slot)
    for i in range(halves):
        loads[i].wait()
        image_rows(i, offset, fs, xb, m["mbuf"], m["mh"], m["ml"], m["bh"], m["bl"], m["ph"], m["plo"])

    waits = []

    def chan_copy(src, dst, send, recv, d):
        copy = pltpu.make_async_remote_copy(
            src_ref=src, dst_ref=dst, send_sem=send.at[d - 1], recv_sem=recv.at[d - 1],
            device_id={"chan": flipped_all(mz, d)}, device_id_type=MESH,
        )
        copy.start()
        waits.append(copy)
        return copy

    orders = [[0] + list(range(1, bits)), [0] + list(range(bits - 1, 0, -1))]
    blk, acc, recv = m["blk"], m["acc"], m["recv"]
    source = {(r, p): blk for r in range(1 << bits) for p in range(2)}
    copies = {}

    def send(r, p, bit):
        copy = pltpu.make_async_remote_copy(
            src_ref=source[r, p].at[r, p],
            dst_ref=recv.at[r, p],
            send_sem=m["rs_send"].at[r, p],
            recv_sem=m["rs_recv"].at[r, p],
            device_id={"facet": flipped(me, bit)},
            device_id_type=MESH,
        )
        copy.start()
        copies[r, p] = copy
        waits.append(copy)

    def ranked(members, later):
        return sorted(members, key=lambda r: [-((r >> b) & 1) for b in later])

    for p in range(2):
        subgrid_plane(p, subs, m["ah"], m["al"], m["ph"], m["plo"], m["grids"])
        for r in range(subs):
            blk[r, p] = m["grids"][subgrid_of[r], p]
        if p == 0:
            pl.semaphore_wait(barrier, bits + parts - 1)
        for r in ranked([r for r in range(subs) if (r >> orders[p][0]) & 1], orders[p][1:]):
            send(r, p, orders[p][0])
    small = [chan_copy(m["tile"], m["offs"].at[d - 1], m["off_send"], m["off_recv"], d) for d in range(1, parts)]

    build_adjoint(fs, share, row_pix, col_pix, mz, m["cbh"], m["cbl"], m["cah"], m["cal"])
    build_hot(bins_ref, m["hot_u"], m["hot_v"])

    members = [list(range(1 << bits)) for _ in range(2)]
    for i in range(bits):
        kept = []
        for p in range(2):
            bit = orders[p][i]
            members[p] = ranked([r for r in members[p] if not (r >> bit) & 1], orders[p][i + 1:])
            kept.append(members[p])
        for pair in zip(*kept):
            for p in range(2):
                r, bit = pair[p], orders[p][i]
                copies[r | (1 << bit), p].wait_recv()
                acc[r, p] = source[r, p][r, p] + recv[r | (1 << bit), p]
                source[r, p] = acc
                if i < bits - 1 and (r >> orders[p][i + 1]) & 1:
                    send(r, p, orders[p][i + 1])

    zsend, zrecv, offs = m["zsend"], m["zrecv"], m["offs"]
    gbufs = [m["gbuf%d" % d] for d in range(parts)]
    misfit_blocks(count_ref, acc.at[0], obs_ref, bins_ref, zsend, m["lhs"], m["hot_u"], m["hot_v"], m["sides"])

    first = [chan_copy(zsend.at[flipped_all(mz, d)], zrecv.at[d - 1], m["z_send"], m["z_recv"], d) for d in range(1, parts)]
    plain = zsend[mz]
    scaled = offset * plain
    for d in range(1, parts):
        small[d - 1].wait_recv()
        first[d - 1].wait_recv()
        block = zrecv[d - 1]
        plain += block
        scaled += offs[d - 1, :1, :] * block
    gbufs[0][0, 0] = plain
    gbufs[0][0, 1] = scaled

    spread_orders = [list(range(1, bits)) + [0], list(range(bits - 1, 0, -1)) + [0]]
    landed = {}

    def spread(d, j, r, start):
        for i in range(start, bits):
            bit = spread_orders[j][i]
            to = r | (1 << bit)
            copy = pltpu.make_async_remote_copy(
                src_ref=gbufs[d].at[r, j], dst_ref=gbufs[d].at[to, j],
                send_sem=m["ag_send"].at[d, j, to], recv_sem=m["ag_recv"].at[d, j, to],
                device_id={"facet": flipped(me, bit)}, device_id_type=MESH,
            )
            copy.start()
            landed[d, j, to] = copy
            waits.append(copy)

    second = [chan_copy(gbufs[0].at[0], gbufs[d].at[0], m["t_send"], m["t_recv"], d) for d in range(1, parts)]
    for j in range(2):
        spread(0, j, 0, 0)
    for tau in range(1, parts + bits + 1):
        if tau < parts:
            second[tau - 1].wait_recv()
            for j in range(2):
                spread(tau, j, 0, 0)
        for i in range(bits):
            d = tau - 1 - i
            if not 0 <= d < parts:
                continue
            for k in range(1 << i):
                for j in range(2):
                    held = sum(1 << spread_orders[j][e] for e in range(i) if (k >> e) & 1)
                    r = held | (1 << spread_orders[j][i])
                    landed[d, j, r].wait_recv()
                    spread(d, j, r, i + 1)
        done = tau - bits
        if 0 <= done < parts:
            adjoint_rows(subs, slots, flipped_all(mz, done), gbufs[done], m["rh"], m["rl"])
    adjoint_images(
        share, fs, out_ref, m["cbh"], m["cbl"], m["cah"], m["cal"], m["rh"], m["rl"], m["wh"], m["wl"]
    )
    for copy in waits:
        copy.wait_send()


def solution(mesh):
    facets, parts = mesh.shape["facet"], mesh.shape["chan"]
    bits = facets.bit_length() - 1

    def on_device(model_taylor, channel_offset, assignment, observed, uv_bins, vis_counts):
        subs, fs = assignment.shape[0], model_taylor.shape[-1]
        share, rows, halves = fs // parts, XM // parts, 2
        xb = fs // halves
        cells, total = SUB_COLS * XM, subs // SUB_COLS * XM
        vmem, dma = pltpu.VMEM, pltpu.SemaphoreType.DMA
        scratch = {
            "mbuf": vmem((halves, 2, 2, xb, fs), F32),
            "tile": vmem((8, XM), F32),
            "offs": vmem((parts - 1, 8, XM), F32),
            "grids": vmem((subs, 2, XM, XM), F32),
            "blk": vmem((subs, 2, XM, XM), F32),
            "acc": vmem((subs, 2, XM, XM), F32),
            "recv": vmem((subs, 2, XM, XM), F32),
            "lhs": vmem((2 * XM, 2 * XM), BF16),
            "hot_u": vmem((2 * XM, uv_bins.shape[-1]), BF16),
            "hot_v": vmem((XM, uv_bins.shape[-1]), BF16),
            "sides": vmem((4 * XM, uv_bins.shape[-1]), BF16),
            "zsend": vmem((parts, 2, rows, XM), F32),
            "zrecv": vmem((parts - 1, 2, rows, XM), F32),
        }
        for d in range(parts):
            scratch["gbuf%d" % d] = vmem((facets, 2, 2, rows, XM), F32)
        for high, low, shape in (
            ("bh", "bl", (2 * fs, 2 * cells)),
            ("ah", "al", (total, 2 * fs)),
            ("mh", "ml", (xb, 2 * fs)),
            ("ph", "plo", (2 * fs, 2 * cells)),
            ("cbh", "cbl", (2 * cells, 2 * fs)),
            ("cah", "cal", (share, 2 * total)),
            ("rh", "rl", (2 * total, 4 * cells)),
            ("wh", "wl", (2 * share, 2 * cells)),
        ):
            scratch[high] = vmem(shape, BF16)
            scratch[low] = vmem(shape, BF16)
        scratch["load_sem"] = dma((halves,))
        scratch["rs_send"] = scratch["rs_recv"] = dma((facets, 2))
        for name in ("off", "z", "t"):
            scratch[name + "_send"] = scratch[name + "_recv"] = dma((parts - 1,))
        scratch["ag_send"] = scratch["ag_recv"] = dma((parts, 2, facets))
        return pl.pallas_call(
            functools.partial(cycle_kernel, list(scratch), bits, parts),
            out_shape=jax.ShapeDtypeStruct((2, 1, 2, share, fs), F32),
            in_specs=[SMEM_SPEC] * 3 + [pl.BlockSpec(memory_space=pl.ANY)] + [VMEM_SPEC] * 2,
            out_specs=VMEM_SPEC,
            scratch_shapes=list(scratch.values()),
            compiler_params=pltpu.CompilerParams(
                collective_id=0, has_side_effects=True, vmem_limit_bytes=VMEM_LIMIT
            ),
        )(assignment, channel_offset, vis_counts, model_taylor, observed, uv_bins)

    return jax.shard_map(
        on_device,
        mesh=mesh,
        in_specs=(
            P(None, "facet", None, None, None),
            P("chan"),
            P(),
            P("chan", "facet", None, None),
            P("chan", "facet", None),
            P("chan", "facet"),
        ),
        out_specs=P(None, "facet", None, "chan", None),
        check_vma=False,
    )
```

```python
import functools

import jax
import jax.numpy as jnp
from jax import lax
from jax.experimental import pallas as pl
from jax.experimental.pallas import tpu as pltpu
from jax.sharding import PartitionSpec as P

XM = 128
FACET_COLS = 4
SUB_COLS = 4
IMAGE = 2048
TWO_PI = 6.283185307179586
F32 = jnp.float32
BF16 = jnp.bfloat16
MESH = pl.DeviceIdType.MESH
VMEM_SPEC = pl.BlockSpec(memory_space=pltpu.VMEM)
SMEM_SPEC = pl.BlockSpec(memory_space=pltpu.SMEM)
VMEM_LIMIT = 56 * 1024 * 1024


def cos_sin(turns):
    quarter = IMAGE // 4
    shift = quarter.bit_length() - 1
    step = (turns + quarter // 2) >> shift
    rest = turns - (step << shift)
    t = rest.astype(F32) * (TWO_PI / IMAGE)
    t2 = t * t
    s = t * (1.0 + t2 * (-1.0 / 6 + t2 * (1.0 / 120 + t2 * (-1.0 / 5040 + t2 * (1.0 / 362880)))))
    c = 1.0 + t2 * (-0.5 + t2 * (1.0 / 24 + t2 * (-1.0 / 720 + t2 * (1.0 / 40320))))
    odd = (step & 1) == 1
    cos = jnp.where(odd, s, c)
    sin = jnp.where(odd, c, s)
    cos = jnp.where(((step + 1) & 2) == 2, -cos, cos)
    sin = jnp.where((step & 2) == 2, -sin, sin)
    return cos, sin


def window(positions, length):
    cos, _ = cos_sin(((2 * positions + 1 - length) * (IMAGE // (2 * length))) & (IMAGE - 1))
    return (0.55 + 0.45 * cos) * (float(length) ** -0.5)


def phases(frequency, pixel):
    cos, sin = cos_sin((frequency * pixel) & (IMAGE - 1))
    return cos, -sin


def split(value):
    high = value.astype(BF16)
    return high, (value - high.astype(F32)).astype(BF16)


def put(high_ref, low_ref, where, value):
    high, low = split(value)
    high_ref[where] = high
    low_ref[where] = low


def dot3(a_high, a_low, b_high, b_low):
    dot = functools.partial(jnp.dot, preferred_element_type=F32)
    return dot(a_high, b_high) + (dot(a_low, b_high) + dot(a_high, b_low))


def iota(shape, dim):
    return lax.broadcasted_iota(jnp.int32, shape, dim)


def flipped(me, bit):
    size = 1 << bit
    return me + (1 - 2 * ((me // size) % 2)) * size


def flipped_all(me, mask):
    for bit in range(mask.bit_length()):
        if (mask >> bit) & 1:
            me = flipped(me, bit)
    return me


def build_forward(fs, row_pix, col_pix, halves, bh, bl, ah, al):
    cells = bh.shape[1] // 2
    total = ah.shape[0]
    chunk = 64

    @pl.loop(0, fs // chunk)
    def _(k):
        base = pl.multiple_of(k * chunk, chunk)
        y = base + iota((chunk, cells), 0)
        re, im = phases(iota((chunk, cells), 1), col_pix + y)
        w = window(base + iota((chunk, XM), 0), fs)[:, :1]
        re, im = re * w, im * w
        top, low = pl.ds(base, chunk), pl.ds(pl.multiple_of(fs + base, chunk), chunk)
        put(bh, bl, (top, slice(0, cells)), re)
        put(bh, bl, (top, slice(cells, 2 * cells)), im)
        put(bh, bl, (low, slice(0, cells)), -im)
        put(bh, bl, (low, slice(cells, 2 * cells)), re)

    @pl.loop(0, total // chunk)
    def _(k):
        base = pl.multiple_of(k * chunk, chunk)
        x = iota((chunk, fs), 1)
        re, im = phases(base + iota((chunk, fs), 0), row_pix + x)
        w = window(iota((8, fs), 1), fs)[:1]
        rows = pl.ds(base, chunk)
        put(ah, al, (rows, slice(0, fs)), re * w)
        put(ah, al, (rows, slice(fs, 2 * fs)), im * w)


def build_adjoint(fs, share, row_pix, col_pix, mz, bh, bl, ah, al):
    cells = bh.shape[0] // 2
    total = ah.shape[1] // 2
    chunk = 64

    @pl.loop(0, cells // chunk)
    def _(k):
        base = pl.multiple_of(k * chunk, chunk)
        re, im = phases(base + iota((chunk, fs), 0), col_pix + iota((chunk, fs), 1))
        w = window(iota((8, fs), 1), fs)[:1]
        re, im = re * w, im * w
        top, low = pl.ds(base, chunk), pl.ds(pl.multiple_of(cells + base, chunk), chunk)
        put(bh, bl, (top, slice(0, fs)), re)
        put(bh, bl, (top, slice(fs, 2 * fs)), -im)
        put(bh, bl, (low, slice(0, fs)), im)
        put(bh, bl, (low, slice(fs, 2 * fs)), re)

    x = mz * share + iota((share, total), 0)
    re, im = phases(iota((share, total), 1), row_pix + x)
    w = window(mz * share + iota((share, XM), 0), fs)[:, :1]
    put(ah, al, (slice(None), slice(0, total)), re * w)
    put(ah, al, (slice(None), slice(total, 2 * total)), im * w)


def image_rows(i, offset, fs, xb, mbuf, mh, ml, bh, bl, ph, plo):
    cells = bh.shape[1] // 2
    for p in range(2):
        value = mbuf[i, 0, p] + offset * mbuf[i, 1, p]
        put(mh, ml, (slice(None), slice(p * fs, (p + 1) * fs)), value)
    tile = 256
    top, low = slice(i * xb, (i + 1) * xb), slice(fs + i * xb, fs + (i + 1) * xb)
    for k in range(2 * cells // tile):
        cols = slice(k * tile, (k + 1) * tile)
        part = dot3(mh[...], ml[...], bh[:, cols], bl[:, cols])
        high, small = split(part)
        ph[top, cols] = high
        plo[top, cols] = small
        if k * tile < cells:
            other = slice(k * tile + cells, (k + 1) * tile + cells)
        else:
            other = slice(k * tile - cells, (k + 1) * tile - cells)
            high, small = -high, -small
        ph[low, other] = high
        plo[low, other] = small


def subgrid_plane(p, subs, ah, al, ph, plo, out):
    cells = ph.shape[1] // 2
    tile = 256
    for k in range(cells // tile):
        part = dot3(
            ah[...], al[...],
            ph[:, p * cells + k * tile:p * cells + (k + 1) * tile],
            plo[:, p * cells + k * tile:p * cells + (k + 1) * tile],
        )
        for a in range(subs // SUB_COLS):
            for b in range(tile // XM):
                s = a * SUB_COLS + k * (tile // XM) + b
                out[s, p] = part[a * XM:(a + 1) * XM, b * XM:(b + 1) * XM]


def build_hot(bins_ref, hot_u, hot_v):
    slots = bins_ref.shape[-1]
    chunk = 512

    @pl.loop(0, slots // chunk)
    def _(k):
        here = pl.ds(pl.multiple_of(k * chunk, chunk), chunk)
        bins = bins_ref[0, :, here]
        cell = iota((XM, chunk), 0)
        at_u = jnp.where(cell == (bins >> 7), 1.0, 0.0).astype(BF16)
        hot_u[:XM, here] = at_u
        hot_u[XM:, here] = at_u
        hot_v[:, here] = jnp.where(cell == (bins & (XM - 1)), 1.0, 0.0).astype(BF16)


def misfit_blocks(count_ref, grid_ref, obs_ref, bins_ref, out_ref, lhs, hot_u, hot_v, sides):
    slots = bins_ref.shape[-1]
    parts, _, rows, _ = out_ref.shape
    for p in range(2):
        high, low = split(grid_ref[p].T)
        lhs[p * XM:(p + 1) * XM, :XM] = high
        lhs[p * XM:(p + 1) * XM, XM:] = low
    count = count_ref[0, 0]
    chunk = 512
    for k in range(slots // chunk):
        here = slice(k * chunk, (k + 1) * chunk)
        at_v = iota((XM, chunk), 0) == (bins_ref[0, :, here] & (XM - 1))
        picked = jnp.dot(lhs[...], hot_u[:, here], preferred_element_type=F32)
        live = k * chunk + iota((1, chunk), 1) < count
        ones = hot_v[:, here]
        for p in range(2):
            predicted = jnp.sum(jnp.where(at_v, picked[p * XM:(p + 1) * XM], 0.0), axis=0, keepdims=True)
            misfit = jnp.where(live, obs_ref[0, 0, p:p + 1, here] - predicted, 0.0)
            high, low = split(misfit)
            sides[2 * p * XM:(2 * p + 1) * XM, here] = ones * high
            sides[(2 * p + 1) * XM:(2 * p + 2) * XM, here] = ones * low

    for p in range(2):
        both = lax.dot_general(
            hot_u[:XM, :], sides[2 * p * XM:(2 * p + 2) * XM, :], (((1,), (1,)), ((), ())),
            preferred_element_type=F32,
        )
        value = both[:, :XM] + both[:, XM:]
        for q in range(parts):
            out_ref[q, p] = value[q * rows:(q + 1) * rows]


def adjoint_rows(subs, slots, q, in_ref, rh, rl):
    rows = in_ref.shape[-2]
    cells = SUB_COLS * XM
    total = rh.shape[0] // 2
    for s in range(subs):
        a, b = s // SUB_COLS, s % SUB_COLS
        top = pl.ds(pl.multiple_of(a * XM + q * rows, rows), rows)
        low = pl.ds(pl.multiple_of(total + a * XM + q * rows, rows), rows)
        for j in range(2):
            left = slice(2 * j * cells + b * XM, 2 * j * cells + (b + 1) * XM)
            right = slice((2 * j + 1) * cells + b * XM, (2 * j + 1) * cells + (b + 1) * XM)
            high, small = split(in_ref[slots[s], j, 0])
            rh[top, left] = high
            rl[top, left] = small
            rh[low, right] = -high
            rl[low, right] = -small
            high, small = split(in_ref[slots[s], j, 1])
            rh[top, right] = high
            rl[top, right] = small
            rh[low, left] = high
            rl[low, left] = small


def adjoint_images(share, fs, out_ref, bh, bl, ah, al, rh, rl, wh, wl):
    cells = SUB_COLS * XM
    tile = 256
    for k in range(4 * cells // tile):
        cols = slice(k * tile, (k + 1) * tile)
        part = dot3(ah[...], al[...], rh[:, cols], rl[:, cols])
        j, rest = k * tile // (2 * cells), k * tile % (2 * cells)
        put(wh, wl, (slice(j * share, (j + 1) * share), slice(rest, rest + tile)), part)
    for k in range(2 * fs // tile):
        cols = slice(k * tile, (k + 1) * tile)
        part = dot3(wh[...], wl[...], bh[:, cols], bl[:, cols])
        p, rest = k * tile // fs, k * tile % fs
        for j in range(2):
            out_ref[j, 0, p, :, rest:rest + tile] = part[j * share:(j + 1) * share]


def cycle_kernel(
    names, bits, parts, assign_ref, off_ref, count_ref, model_ref, obs_ref, bins_ref, out_ref, *scratch
):
    m = dict(zip(names, scratch))
    me, mz = lax.axis_index("facet"), lax.axis_index("chan")
    subs, fs, share = assign_ref.shape[0], model_ref.shape[-1], out_ref.shape[3]
    halves, xb = m["mbuf"].shape[0], m["mbuf"].shape[3]
    row_pix, col_pix = (me // FACET_COLS) * fs, (me % FACET_COLS) * fs

    loads = []
    for i in range(halves):
        load = pltpu.make_async_copy(
            model_ref.at[:, 0, :, pl.ds(i * xb, xb), :], m["mbuf"].at[i], m["load_sem"].at[i]
        )
        load.start()
        loads.append(load)
    barrier = pltpu.get_barrier_semaphore()
    for b in range(bits):
        pl.semaphore_signal(barrier, inc=1, device_id={"facet": flipped(me, b)}, device_id_type=MESH)
    for d in range(1, parts):
        pl.semaphore_signal(barrier, inc=1, device_id={"chan": flipped_all(mz, d)}, device_id_type=MESH)

    offset = off_ref[0]
    m["tile"][...] = jnp.full(m["tile"].shape, offset, F32)
    build_forward(fs, row_pix, col_pix, halves, m["bh"], m["bl"], m["ah"], m["al"])
    subgrid_of = [assign_ref[flipped_all(me, r)] for r in range(subs)]
    slots = []
    for s in range(subs):
        slot = jnp.int32(0)
        for r in range(1, subs):
            slot = jnp.where(subgrid_of[r] == s, r, slot)
        slots.append(slot)
    for i in range(halves):
        loads[i].wait()
        image_rows(i, offset, fs, xb, m["mbuf"], m["mh"], m["ml"], m["bh"], m["bl"], m["ph"], m["plo"])

    waits = []

    def chan_copy(src, dst, send, recv, d):
        copy = pltpu.make_async_remote_copy(
            src_ref=src, dst_ref=dst, send_sem=send.at[d - 1], recv_sem=recv.at[d - 1],
            device_id={"chan": flipped_all(mz, d)}, device_id_type=MESH,
        )
        copy.start()
        waits.append(copy)
        return copy

    orders = [[0] + list(range(1, bits)), [0] + list(range(bits - 1, 0, -1))]
    blk, acc, recv = m["blk"], m["acc"], m["recv"]
    source = {(r, p): blk for r in range(1 << bits) for p in range(2)}
    copies = {}

    def send(r, p, bit):
        copy = pltpu.make_async_remote_copy(
            src_ref=source[r, p].at[r, p],
            dst_ref=recv.at[r, p],
            send_sem=m["rs_send"].at[r, p],
            recv_sem=m["rs_recv"].at[r, p],
            device_id={"facet": flipped(me, bit)},
            device_id_type=MESH,
        )
        copy.start()
        copies[r, p] = copy
        waits.append(copy)

    def ranked(members, later):
        return sorted(members, key=lambda r: [-((r >> b) & 1) for b in later])

    for p in range(2):
        subgrid_plane(p, subs, m["ah"], m["al"], m["ph"], m["plo"], m["grids"])
        for r in range(subs):
            blk[r, p] = m["grids"][subgrid_of[r], p]
        if p == 0:
            pl.semaphore_wait(barrier, bits + parts - 1)
        for r in ranked([r for r in range(subs) if (r >> orders[p][0]) & 1], orders[p][1:]):
            send(r, p, orders[p][0])
    small = [chan_copy(m["tile"], m["offs"].at[d - 1], m["off_send"], m["off_recv"], d) for d in range(1, parts)]

    members = [list(range(1 << bits)) for _ in range(2)]
    for i in range(bits):
        kept = []
        for p in range(2):
            bit = orders[p][i]
            members[p] = ranked([r for r in members[p] if not (r >> bit) & 1], orders[p][i + 1:])
            kept.append(members[p])
        for pair in zip(*kept):
            for p in range(2):
                r, bit = pair[p], orders[p][i]
                copies[r | (1 << bit), p].wait_recv()
                acc[r, p] = source[r, p][r, p] + recv[r | (1 << bit), p]
                source[r, p] = acc
                if i < bits - 1 and (r >> orders[p][i + 1]) & 1:
                    send(r, p, orders[p][i + 1])
        if i == 0:
            build_hot(bins_ref, m["hot_u"], m["hot_v"])

    zsend, zrecv, offs = m["zsend"], m["zrecv"], m["offs"]
    gbufs = [m["gbuf%d" % d] for d in range(parts)]
    misfit_blocks(count_ref, acc.at[0], obs_ref, bins_ref, zsend, m["lhs"], m["hot_u"], m["hot_v"], m["sides"])

    first = [chan_copy(zsend.at[flipped_all(mz, d)], zrecv.at[d - 1], m["z_send"], m["z_recv"], d) for d in range(1, parts)]
    build_adjoint(fs, share, row_pix, col_pix, mz, m["cbh"], m["cbl"], m["cah"], m["cal"])
    plain = zsend[mz]
    scaled = offset * plain
    for d in range(1, parts):
        small[d - 1].wait_recv()
        first[d - 1].wait_recv()
        block = zrecv[d - 1]
        plain += block
        scaled += offs[d - 1, :1, :] * block
    gbufs[0][0, 0] = plain
    gbufs[0][0, 1] = scaled

    spread_orders = [list(range(1, bits)) + [0], list(range(bits - 1, 0, -1)) + [0]]
    landed = {}

    def spread(d, j, r, start):
        for i in range(start, bits):
            bit = spread_orders[j][i]
            to = r | (1 << bit)
            copy = pltpu.make_async_remote_copy(
                src_ref=gbufs[d].at[r, j], dst_ref=gbufs[d].at[to, j],
                send_sem=m["ag_send"].at[d, j, to], recv_sem=m["ag_recv"].at[d, j, to],
                device_id={"facet": flipped(me, bit)}, device_id_type=MESH,
            )
            copy.start()
            landed[d, j, to] = copy
            waits.append(copy)

    second = [chan_copy(gbufs[0].at[0], gbufs[d].at[0], m["t_send"], m["t_recv"], d) for d in range(1, parts)]
    for j in range(2):
        spread(0, j, 0, 0)
    for tau in range(1, parts + bits + 1):
        if tau < parts:
            second[tau - 1].wait_recv()
            for j in range(2):
                spread(tau, j, 0, 0)
        for i in range(bits):
            d = tau - 1 - i
            if not 0 <= d < parts:
                continue
            for k in range(1 << i):
                for j in range(2):
                    held = sum(1 << spread_orders[j][e] for e in range(i) if (k >> e) & 1)
                    r = held | (1 << spread_orders[j][i])
                    landed[d, j, r].wait_recv()
                    spread(d, j, r, i + 1)
        done = tau - bits
        if 0 <= done < parts:
            adjoint_rows(subs, slots, flipped_all(mz, done), gbufs[done], m["rh"], m["rl"])
    adjoint_images(
        share, fs, out_ref, m["cbh"], m["cbl"], m["cah"], m["cal"], m["rh"], m["rl"], m["wh"], m["wl"]
    )
    for copy in waits:
        copy.wait_send()


def solution(mesh):
    facets, parts = mesh.shape["facet"], mesh.shape["chan"]
    bits = facets.bit_length() - 1

    def on_device(model_taylor, channel_offset, assignment, observed, uv_bins, vis_counts):
        subs, fs = assignment.shape[0], model_taylor.shape[-1]
        share, rows, halves = fs // parts, XM // parts, 2
        xb = fs // halves
        cells, total = SUB_COLS * XM, subs // SUB_COLS * XM
        vmem, dma = pltpu.VMEM, pltpu.SemaphoreType.DMA
        scratch = {
            "mbuf": vmem((halves, 2, 2, xb, fs), F32),
            "tile": vmem((8, XM), F32),
            "offs": vmem((parts - 1, 8, XM), F32),
            "grids": vmem((subs, 2, XM, XM), F32),
            "blk": vmem((subs, 2, XM, XM), F32),
            "acc": vmem((subs, 2, XM, XM), F32),
            "recv": vmem((subs, 2, XM, XM), F32),
            "lhs": vmem((2 * XM, 2 * XM), BF16),
            "hot_u": vmem((2 * XM, uv_bins.shape[-1]), BF16),
            "hot_v": vmem((XM, uv_bins.shape[-1]), BF16),
            "sides": vmem((4 * XM, uv_bins.shape[-1]), BF16),
            "zsend": vmem((parts, 2, rows, XM), F32),
            "zrecv": vmem((parts - 1, 2, rows, XM), F32),
        }
        for d in range(parts):
            scratch["gbuf%d" % d] = vmem((facets, 2, 2, rows, XM), F32)
        for high, low, shape in (
            ("bh", "bl", (2 * fs, 2 * cells)),
            ("ah", "al", (total, 2 * fs)),
            ("mh", "ml", (xb, 2 * fs)),
            ("ph", "plo", (2 * fs, 2 * cells)),
            ("cbh", "cbl", (2 * cells, 2 * fs)),
            ("cah", "cal", (share, 2 * total)),
            ("rh", "rl", (2 * total, 4 * cells)),
            ("wh", "wl", (2 * share, 2 * cells)),
        ):
            scratch[high] = vmem(shape, BF16)
            scratch[low] = vmem(shape, BF16)
        scratch["load_sem"] = dma((halves,))
        scratch["rs_send"] = scratch["rs_recv"] = dma((facets, 2))
        for name in ("off", "z", "t"):
            scratch[name + "_send"] = scratch[name + "_recv"] = dma((parts - 1,))
        scratch["ag_send"] = scratch["ag_recv"] = dma((parts, 2, facets))
        return pl.pallas_call(
            functools.partial(cycle_kernel, list(scratch), bits, parts),
            out_shape=jax.ShapeDtypeStruct((2, 1, 2, share, fs), F32),
            in_specs=[SMEM_SPEC] * 3 + [pl.BlockSpec(memory_space=pl.ANY)] + [VMEM_SPEC] * 2,
            out_specs=VMEM_SPEC,
            scratch_shapes=list(scratch.values()),
            compiler_params=pltpu.CompilerParams(
                collective_id=0, has_side_effects=True, vmem_limit_bytes=VMEM_LIMIT
            ),
        )(assignment, channel_offset, vis_counts, model_taylor, observed, uv_bins)

    return jax.shard_map(
        on_device,
        mesh=mesh,
        in_specs=(
            P(None, "facet", None, None, None),
            P("chan"),
            P(),
            P("chan", "facet", None, None),
            P("chan", "facet", None),
            P("chan", "facet"),
        ),
        out_specs=P(None, "facet", None, "chan", None),
        check_vma=False,
    )
```
